32 devices in a mesh: grid: 8 (over z, core), tp: 4 (over y, x).
Axes of the slice: x: 2, y: 2, z: 4, core: 2. Of those that a mesh axis runs over, the one named last changes fastest.
Arguments:
- latents: bfloat16 [3072, 3072], P('grid'), may hold values from -6 to 6
- input_weight: bfloat16 [3072, 1536], P('grid', 'tp'), as said below
- norm_gains: float32 [2, 128], replicated, as said below
- text_pairs: bfloat16 [256, 1024], P(None, 'tp'), may hold values from -6 to 6
- text_count: int32 [1], replicated, may hold values from 64 to 256
- output_weight: bfloat16 [512, 3072], P('tp', 'grid'), may hold values from -0.25 to 0.25
Outputs:
- block_output: bfloat16 [3072, 3072], P('grid', 'tp')
The draws below stay inside these ranges and needn't reach their ends.
Inputs may be any that keep to these rules, and one draw needn't show every extreme that they name: `text_count`: number of valid text tokens; the remaining text slots are padding. `input_weight`: a projection scaled by its fan-in. `norm_gains`: positive gains.
All inputs are finite; a program needn't handle non-finite values.
Results may differ from the reference program's by a relative error of at most 0.015.
Values may be sent and summed in bfloat16 or wider, within the bound.
No kernel may reach another device: no remote copies, remote signals or barrier semaphores. Data moves between devices by JAX's collectives and lax.ppermute only.
A program may use at most 64 MiB of HBM per device.

```python
import jax
import jax.numpy as jnp
import numpy as np
from jax import lax

D = 3072
HD = 128
TXT = 256
HEAD_DEV = 1
GRID_H = 4
WT = 1
TILE = 384
HEADS = 4
TOKENS = 3072
N_TP = 4


def draw_input_weight(key, part):
    first_key = jax.random.fold_in(key, 11)
    basis = jax.random.normal(first_key, (D, HEADS, 3, HD), jnp.float32) * D ** (-0.5)
    return basis.reshape(D, 3 * HEADS * HD).astype(jnp.bfloat16)


def draw_norm_gains(key, part):
    gain_key = jax.random.fold_in(key, 21)
    return jax.random.uniform(gain_key, (2, HD), jnp.float32, 0.6, 1.6)


def levels(rng, shape, shards, smallest, largest):
    level, own = 1.0, jax.random.fold_in(rng, 6)
    for axis_at, parts in shards:
        heights = jnp.exp(jax.random.uniform(jax.random.fold_in(own, axis_at), (parts,), jnp.float32, smallest / len(shards), largest / len(shards)))
        level = level * jnp.repeat(heights, shape[axis_at] // parts).reshape([-1 if axis == axis_at else 1 for axis in range(len(shape))])
    return level


def centred(rng, extent, spread, bound, shards=(), kind=jnp.bfloat16):
    factor_of = levels(rng, extent, shards, -0.22, 0.18) if shards else 1.0
    entries = jax.random.normal(rng, extent, jnp.float32) * spread * factor_of
    return jnp.minimum(jnp.maximum(entries, -bound), bound).astype(kind)


def setup_inputs(seed: int = 0) -> dict:
    keys = jax.random.split(jax.random.key(seed), 7)
    latents = centred(keys[0], (TOKENS, D), 1.0, 6.0, ((0, 8),))
    input_weight = draw_input_weight(jax.random.fold_in(keys[6], 71), 0)
    norm_gains = draw_norm_gains(jax.random.fold_in(keys[6], 71), 0)
    text_pairs = centred(keys[3], (TXT, 2 * HEADS * HD), 1.0, 6.0, ((1, 4),))
    text_count = jax.random.randint(keys[4], (1,), TXT // 4, TXT + 1).astype(jnp.int32)
    output_weight = centred(keys[5], (HEADS * HD, D), (HEADS * HD) ** -0.5, 0.25, ((0, 4), (1, 8)))
    return dict(latents=latents, input_weight=input_weight, norm_gains=norm_gains, text_pairs=text_pairs, text_count=text_count, output_weight=output_weight)


epsilon = 1e-06

def root_norm(values, gain):
    return values * lax.rsqrt(lax.optimization_barrier(jnp.mean(values * values, axis=-1, keepdims=True)) + epsilon) * gain

def reference(latents, input_weight, norm_gains, text_pairs, text_count, output_weight):
    projected = jnp.dot(latents, input_weight, preferred_element_type=jnp.float32).reshape(TOKENS, HEADS, 3, HD)
    queries = root_norm(projected[:, :, 0], norm_gains[0]).astype(jnp.bfloat16)
    key_rows = root_norm(projected[:, :, 1], norm_gains[1]).astype(jnp.bfloat16)
    values = projected[:, :, 2].astype(jnp.bfloat16)
    text = text_pairs.reshape(TXT, HEADS, 2, HD)
    text_keys = root_norm(text[:, :, 0].astype(jnp.float32), norm_gains[1]).astype(jnp.bfloat16)
    text_values = text[:, :, 1]
    grid_time = TOKENS // (TILE * GRID_H * WT)
    width_keep = min(3, WT)
    starts = np.clip(np.arange(WT) - 1, 0, WT - width_keep)
    width_index = starts[:, None] + np.arange(width_keep)[None, :]
    width_ok = np.abs(width_index - np.arange(WT)[:, None]) <= 1
    offsets = [(step_time, step_height) for step_time in (-1, 0, 1) for step_height in (-1, 0, 1)]
    time_pos = jnp.arange(grid_time)
    height_pos = jnp.arange(GRID_H)
    plane_ok = jnp.stack([(time_pos[:, None] + step_time >= 0) & (time_pos[:, None] + step_time < grid_time) & ((height_pos[None, :] + step_height >= 0) & (height_pos[None, :] + step_height < GRID_H)) for step_time, step_height in offsets])
    live = plane_ok[:, :, :, None, None, None] & jnp.asarray(width_ok)[None, None, None, :, :, None]
    live = jnp.broadcast_to(live, (9, grid_time, GRID_H, WT, width_keep, TILE))
    live = live.transpose(1, 2, 3, 0, 4, 5).reshape(grid_time, GRID_H, WT, 9 * width_keep * TILE)
    live_text = jnp.arange(TXT) < text_count[0]
    score_scale = HD ** (-0.5)

    def windows(rows):
        tiles = rows.reshape(grid_time, GRID_H, WT, TILE, HD)
        padded = jnp.pad(tiles, ((1, 1), (1, 1), (0, 0), (0, 0), (0, 0)))
        stacked = jnp.stack([padded[1 + step_time:1 + step_time + grid_time, 1 + step_height:1 + step_height + GRID_H] for step_time, step_height in offsets])
        chosen = stacked[:, :, :, width_index]
        return chosen.transpose(1, 2, 3, 0, 4, 5, 6).reshape(grid_time, GRID_H, WT, 9 * width_keep * TILE, HD).astype(jnp.float32)

    def one_head(operands):
        query_head, key_head, value_head, text_key, text_value = operands
        query_tiles = query_head.reshape(grid_time, GRID_H, WT, TILE, HD).astype(jnp.float32)
        key_window = windows(key_head)
        value_window = windows(value_head)
        video_scores = jnp.einsum('abwqd,abwkd->abwqk', query_tiles, key_window) * score_scale
        text_scores = jnp.einsum('abwqd,kd->abwqk', query_tiles, text_key.astype(jnp.float32)) * score_scale
        video_scores = jnp.where(live[:, :, :, None, :], video_scores, -jnp.inf)
        text_scores = jnp.where(live_text[None, None, None, None, :], text_scores, -jnp.inf)
        row_max = jnp.maximum(video_scores.max(-1), text_scores.max(-1))[..., None]
        video_exp = jnp.exp(video_scores - row_max)
        text_exp = jnp.exp(text_scores - row_max)
        denominator = video_exp.sum(-1, keepdims=True) + text_exp.sum(-1, keepdims=True)
        video_weights = (video_exp / denominator).astype(jnp.bfloat16)
        text_weights = (text_exp / denominator).astype(jnp.bfloat16)
        mixed = jnp.einsum('abwqk,abwkd->abwqd', video_weights.astype(jnp.float32), value_window)
        mixed = mixed + jnp.einsum('abwqk,kd->abwqd', text_weights.astype(jnp.float32), text_value.astype(jnp.float32))
        return mixed.astype(jnp.bfloat16).reshape(TOKENS, HD)
    per_head = lax.map(one_head, (queries.transpose(1, 0, 2), key_rows.transpose(1, 0, 2), values.transpose(1, 0, 2), text_keys.transpose(1, 0, 2), text_values.transpose(1, 0, 2)))
    attention = per_head.transpose(1, 0, 2).reshape(TOKENS, HEADS * HD)
    group_width = HEAD_DEV * HD
    summed = jnp.zeros((TOKENS, D), jnp.float32)
    for group in range(N_TP):
        partial_term = jnp.dot(attention[:, group * group_width:(group + 1) * group_width], output_weight[group * group_width:(group + 1) * group_width], preferred_element_type=jnp.float32).astype(jnp.bfloat16)
        partial_term = lax.optimization_barrier(partial_term)
        summed = summed + partial_term.astype(jnp.float32)
    return summed.astype(jnp.bfloat16)
```

```python
import functools

import jax
import jax.numpy as jnp
import numpy as np
from jax import lax
from jax.experimental import pallas as pl
from jax.experimental.pallas import tpu as pltpu
from jax.sharding import PartitionSpec as P

GRID_H = 4
TILE = 384
LOG2E = float(np.log2(np.e))

epsilon = 1e-06


F32 = jnp.float32
BF16 = jnp.bfloat16
VMEM = pl.BlockSpec(memory_space=pltpu.VMEM)
SMEM = pl.BlockSpec(memory_space=pltpu.SMEM)


def shape_of(shape, dtype):
    return jax.ShapeDtypeStruct(shape, dtype)


def cost(flops, bytes_accessed, transcendentals=0):
    return pl.CostEstimate(
        flops=int(flops), bytes_accessed=int(bytes_accessed), transcendentals=int(transcendentals)
    )


def root_norm(values, gain):
    return values * lax.rsqrt(jnp.mean(values * values, axis=-1, keepdims=True) + epsilon) * gain


def partial_body(count, carried, block_ref, *refs):
    mine_blocks, refs = refs[:count], refs[count:]
    other_blocks, refs = refs[:count], refs[count:]
    weights, refs = refs[:count], refs[count:]
    mine = other = None
    if carried:
        mine, other = refs[0][...], refs[1][...]
        refs = refs[2:]
    for at in range(count):
        weight = weights[at][...]
        here = jnp.dot(mine_blocks[at][...], weight, preferred_element_type=F32)
        there = jnp.dot(other_blocks[at][...], weight, preferred_element_type=F32)
        mine = here if mine is None else mine + here
        other = there if other is None else other + there
    refs[0][...] = mine
    refs[1][...] = other


def partial_product(blocks, latents, partner_latents, weights, carry):
    count = len(weights)
    rows = latents.shape[0]
    depth, width = weights[0].shape
    column = [
        pl.BlockSpec((rows, depth), lambda step, block, at=at: (0, block[at])) for at in range(count)
    ]
    whole = pl.BlockSpec((depth, width), lambda step, block: (0, 0))
    total = pl.BlockSpec((rows, width), lambda step, block: (0, 0))
    carry = list(carry)
    return pl.pallas_call(
        functools.partial(partial_body, count, bool(carry)),
        out_shape=[shape_of((rows, width), F32)] * 2,
        grid_spec=pltpu.PrefetchScalarGridSpec(
            num_scalar_prefetch=1,
            grid=(1,),
            in_specs=column + column + [whole] * count + [total] * len(carry),
            out_specs=[total] * 2,
        ),
        cost_estimate=cost(
            4 * rows * depth * width * count,
            count * (4 * rows * depth + 2 * depth * width) + 16 * rows * width,
        ),
        name="partial_product",
    )(blocks, *([latents] * count), *([partner_latents] * count), *weights, *carry)


def finish_body(head_size, has_partner, *refs):
    total = refs[0][...]
    if has_partner:
        total = total + refs[1][...]
        refs = refs[1:]
    gains = refs[1][...]
    query_ref, pair_ref = refs[2:]
    query_ref[...] = root_norm(total[:, :head_size], gains[0:1]).astype(BF16)
    keys = root_norm(total[:, head_size : 2 * head_size], gains[1:2])
    pair_ref[:, :head_size] = keys.astype(BF16)
    pair_ref[:, head_size:] = total[:, 2 * head_size :].astype(BF16)


def finish_projection(parts, norm_gains):
    rows, width = parts[0].shape
    head_size = norm_gains.shape[1]
    return pl.pallas_call(
        functools.partial(finish_body, head_size, len(parts) > 1),
        out_shape=[shape_of((rows, head_size), BF16), shape_of((rows, 2 * head_size), BF16)],
        in_specs=[VMEM] * (len(parts) + 1),
        out_specs=[VMEM] * 2,
        cost_estimate=cost(10 * rows * width, 10 * rows * width, 2 * rows),
        name="finish_projection",
    )(*parts, norm_gains)


def project(latents, input_weight, norm_gains):
    devices = lax.axis_size("grid")
    place = lax.axis_index("grid")
    chips = devices // 2
    if devices % 2 or chips > 4:
        weight = lax.all_gather(input_weight, "grid", axis=0, tiled=True)
        total = jnp.dot(latents, weight, preferred_element_type=F32)
        return finish_projection([total], norm_gains)
    chip, core = place // 2, place % 2
    swap = [(at, at ^ 1) for at in range(devices)]
    shards = [input_weight]
    for step in range(1, chips):
        pairs = [(at, (at + 2 * step) % devices) for at in range(devices)]
        shards.append(lax.ppermute(input_weight, "grid", pairs))
    partner_latents = lax.ppermute(latents, "grid", swap)
    blocks = [2 * ((chip - step) % chips) + core for step in range(chips)]
    carry = ()
    split = max(1, chips - 1)
    for first, last in ((0, split), (split, chips)):
        if last > first:
            carry = partial_product(
                jnp.stack(blocks[first:last]).astype(jnp.int32),
                latents,
                partner_latents,
                shards[first:last],
                carry,
            )
    mine, other = carry
    return finish_projection([mine, lax.ppermute(other, "grid", swap)], norm_gains)


def attend(state, query, keys, values, factor, live=None):
    scores = lax.dot_general(query, keys, (((1,), (1,)), ((), ())), preferred_element_type=F32)
    if live is not None:
        scores = jnp.where(live, scores, -jnp.inf)
    top = scores.max(-1, keepdims=True)
    if state is None:
        weights = jnp.exp2((scores - top) * factor)
        mixed = jnp.dot(weights.astype(BF16), values, preferred_element_type=F32)
        return top, weights.sum(-1, keepdims=True), mixed
    old_top, old_sum, old_mixed = state
    top = jnp.maximum(old_top, top)
    fade = jnp.exp2((old_top - top) * factor)
    weights = jnp.exp2((scores - top) * factor)
    mixed = jnp.dot(weights.astype(BF16), values, preferred_element_type=F32)
    return top, old_sum * fade + weights.sum(-1, keepdims=True), old_mixed * fade + mixed


def attend_body(count, gated, with_text, carried, last, factor, *refs):
    flags_ref, query_ref = refs[:2]
    pair_refs, refs = refs[2 : 2 + count], refs[2 + count :]
    head_size = query_ref.shape[1]
    query = query_ref[...]
    rows = query.shape[0]
    state = None
    if with_text:
        text_ref, gains_ref = refs[:2]
        refs = refs[2:]
    if carried:
        state = refs[0][:, 0:1], refs[1][:, 0:1], refs[2][...]
        refs = refs[3:]
    scratch = refs[-3:]
    outs = refs[:-3]
    if with_text:
        text_keys = root_norm(text_ref[:, :head_size].astype(F32), gains_ref[1:2]).astype(BF16)
        live = lax.broadcasted_iota(jnp.int32, (rows, text_ref.shape[0]), 1) < flags_ref[0]
        state = attend(state, query, text_keys, text_ref[:, head_size:], factor, live)
    for at in range(count):
        if gated[at] is None:
            pair = pair_refs[at][...]
            state = attend(state, query, pair[:, :head_size], pair[:, head_size:], factor)
    for at in range(count):
        if gated[at] is not None:
            scratch[0][...], scratch[1][...], scratch[2][...] = state

            @pl.when(flags_ref[gated[at]] > 0)
            def _():
                pair = pair_refs[at][...]
                before = scratch[0][...], scratch[1][...], scratch[2][...]
                after = attend(before, query, pair[:, :head_size], pair[:, head_size:], factor)
                scratch[0][...], scratch[1][...], scratch[2][...] = after

            state = scratch[0][...], scratch[1][...], scratch[2][...]
    top, total, mixed = state
    if last:
        outs[0][...] = (mixed / total).astype(BF16)
    else:
        outs[0][...] = jnp.broadcast_to(top, outs[0].shape)
        outs[1][...] = jnp.broadcast_to(total, outs[1].shape)
        outs[2][...] = mixed


def attention_step(flags, query, pairs, gated, text=None, carry=(), last=False):
    rows, head_size = query.shape
    factor = head_size ** (-0.5) * LOG2E
    extra = list(text) if text is not None else []
    carry = list(carry)
    plane = shape_of((rows, head_size), F32)
    operands = [flags, query, *pairs, *extra, *carry]
    columns = sum(pair.shape[0] for pair in pairs)
    return pl.pallas_call(
        functools.partial(
            attend_body, len(pairs), tuple(gated), text is not None, bool(carry), last, factor
        ),
        out_shape=shape_of((rows, head_size), BF16) if last else [plane] * 3,
        in_specs=[SMEM] + [VMEM] * (len(operands) - 1),
        out_specs=VMEM if last else [VMEM] * 3,
        scratch_shapes=[
            pltpu.VMEM((rows, 1), F32),
            pltpu.VMEM((rows, 1), F32),
            pltpu.VMEM((rows, head_size), F32),
        ],
        cost_estimate=cost(
            4 * rows * columns * head_size, 4 * columns * head_size, rows * columns
        ),
        name="attention_step",
    )(*operands)


def attention_rows(query, pair, text_pairs, norm_gains, text_count):
    devices = lax.axis_size("grid")
    place = lax.axis_index("grid")
    times = devices // GRID_H
    time, height = place // GRID_H, place % GRID_H
    swap = [(at, at ^ 1) for at in range(devices)]
    outer = []
    for at in range(devices):
        row = at % GRID_H
        beyond = row - 1 if row % 2 == 0 else row + 1
        if 0 <= beyond < GRID_H:
            outer.append((at, at - row + beyond))
    beyond = jnp.where(height % 2 == 0, height - 1, height + 1)
    outer_ok = (beyond >= 0) & (beyond < GRID_H)

    def reach(pairs, by):
        table = dict(pairs)
        return [(at, table[at] + by * GRID_H) for at in table if 0 <= table[at] + by * GRID_H < devices]

    if times == 2:
        steps = [None]
    elif times > 2:
        steps = [1, -1]
    else:
        steps = []
    same = [(at, at) for at in range(devices)]
    flags = [text_count[0]]
    plans = []
    for step in steps:
        if step is None:
            along = [(at, (at + GRID_H) % devices) for at in range(devices)]
            across = [(at, (to + GRID_H) % devices) for at, to in outer]
            ok = None
        else:
            along, across = reach(same, step), reach(outer, step)
            ok = (time - step >= 0) & (time - step < times)
        plans.append((along, across, ok))
    far = [lax.ppermute(pair, "grid", along) for along, _, _ in plans]
    near_outer = lax.ppermute(pair, "grid", outer)
    far_outer = [lax.ppermute(pair, "grid", across) for _, across, _ in plans]
    partner = lax.ppermute(pair, "grid", swap)
    flags.append(outer_ok.astype(jnp.int32))
    gates = []
    for _, _, ok in plans:
        if ok is None:
            gates.append((None, 1))
        else:
            flags.append(ok.astype(jnp.int32))
            flags.append((ok & outer_ok).astype(jnp.int32))
            gates.append((len(flags) - 2, len(flags) - 1))
    flags = jnp.stack(flags).astype(jnp.int32)
    carry = attention_step(flags, query, [pair], [None], text=(text_pairs, norm_gains))
    final = not steps
    carry = attention_step(
        flags, query, [partner, near_outer], [None, 1], carry=carry, last=final
    )
    for at, (inner_gate, outer_gate) in enumerate(gates):
        carry = attention_step(
            flags, query, [far[at], far_outer[at]], [inner_gate, outer_gate], carry=carry
        )
        carry = attention_step(
            flags,
            query,
            [lax.ppermute(far[at], "grid", swap)],
            [inner_gate],
            carry=carry,
            last=at == len(gates) - 1,
        )
    return carry


def output_body(groups, order_ref, *refs):
    attention, refs = refs[:groups], refs[groups:]
    mine_ref, other_ref, out_ref, held = refs
    depth, width = mine_ref.shape[0] // groups, mine_ref.shape[1]
    for at in range(groups):
        held[at] = attention[at][...]
    mine = other = None
    for at in range(groups):
        here = jnp.dot(
            held[order_ref[at]], mine_ref[at * depth : (at + 1) * depth], preferred_element_type=F32
        )
        there = jnp.dot(
            held[order_ref[at]], other_ref[at * depth : (at + 1) * depth], preferred_element_type=F32
        )
        mine = here if mine is None else mine + here
        other = there if other is None else other + there
    core = order_ref[groups]

    @pl.when(core == 0)
    def _():
        out_ref[:, :width] = mine.astype(BF16)
        out_ref[:, width:] = other.astype(BF16)

    @pl.when(core != 0)
    def _():
        out_ref[:, :width] = other.astype(BF16)
        out_ref[:, width:] = mine.astype(BF16)


def output_product(order, attention, mine, other):
    groups = len(attention)
    rows, depth = attention[0].shape
    width = mine.shape[1]
    return pl.pallas_call(
        functools.partial(output_body, groups),
        out_shape=shape_of((rows, 2 * width), BF16),
        in_specs=[SMEM] + [VMEM] * (groups + 2),
        out_specs=VMEM,
        scratch_shapes=[pltpu.VMEM((groups, rows, depth), BF16)],
        cost_estimate=cost(
            4 * rows * depth * groups * width, 4 * depth * groups * width + 4 * rows * width
        ),
        name="output_product",
    )(order, *attention, mine, other)


def gather_output_weight(output_weight):
    devices, groups = lax.axis_size("grid"), lax.axis_size("tp")

    def flat(chip, core, group):
        return (2 * chip + core) * groups + group

    pieces = []
    for turn in range(groups):
        pairs = [
            (flat(chip, core, group), flat((group + turn) % groups, core, chip))
            for chip in range(groups)
            for core in range(2)
            for group in range(groups)
        ]
        pieces.append(lax.ppermute(output_weight, ("grid", "tp"), pairs))
    mine = jnp.concatenate(pieces, axis=0)
    swap = [(at, at ^ 1) for at in range(devices)]
    return mine, lax.ppermute(mine, "grid", swap)


def local(latents, input_weight, norm_gains, text_pairs, text_count, output_weight):
    devices, groups = lax.axis_size("grid"), lax.axis_size("tp")
    query, pair = project(latents, input_weight, norm_gains)
    attention = attention_rows(query, pair, text_pairs, norm_gains, text_count)
    if devices == 2 * groups and groups & (groups - 1) == 0:
        mine, other = gather_output_weight(output_weight)
        place, group = lax.axis_index("grid"), lax.axis_index("tp")
        gathered = [attention] + [
            lax.ppermute(attention, "tp", [(at, at ^ by) for at in range(groups)])
            for by in range(1, groups)
        ]
        sources = [(place // 2 - turn) % groups for turn in range(groups)]
        order = jnp.stack([group ^ source for source in sources] + [place % 2]).astype(jnp.int32)
        return output_product(order, gathered, mine, other)
    weight = lax.all_gather(output_weight, "grid", axis=1, tiled=True)
    term = jnp.dot(attention, weight, preferred_element_type=F32)
    return lax.psum_scatter(term.astype(BF16), "tp", scatter_dimension=1, tiled=True)


def solution(mesh):
    placed = (P("grid", None), P("grid", "tp"), P(), P(None, "tp"), P(), P("tp", "grid"))
    return jax.shard_map(
        local, mesh=mesh, in_specs=placed, out_specs=P("grid", "tp"), check_vma=False
    )
```

```python
import functools

import jax
import jax.numpy as jnp
import numpy as np
from jax import lax
from jax.experimental import pallas as pl
from jax.experimental.pallas import tpu as pltpu
from jax.sharding import PartitionSpec as P


GRID_H = 4
LOG2E = float(np.log2(np.e))

epsilon = 1e-06


F32 = jnp.float32
BF16 = jnp.bfloat16
VMEM = pl.BlockSpec(memory_space=pltpu.VMEM)
SMEM = pl.BlockSpec(memory_space=pltpu.SMEM)
GRANT = pltpu.CompilerParams(vmem_limit_bytes=16 * 1024 * 1024)


def shape_of(shape, dtype):
    return jax.ShapeDtypeStruct(shape, dtype)


def cost(flops, bytes_accessed, transcendentals=0):
    return pl.CostEstimate(
        flops=int(flops), bytes_accessed=int(bytes_accessed), transcendentals=int(transcendentals)
    )


def root_norm(values, gain):
    return values * lax.rsqrt(jnp.mean(values * values, axis=-1, keepdims=True) + epsilon) * gain


def partial_body(slots, carried, latents_ref, partner_ref, *refs):
    chips = lax.axis_size("grid") // 2
    place = lax.axis_index("grid")
    chip, core = place // 2, lax.rem(place, 2)
    weights, refs = refs[: len(slots)], refs[len(slots) :]
    if carried:
        carried_mine, carried_other = refs[:2]
        refs = refs[2:]
    mine_ref, other_ref = refs
    depth = weights[0].shape[0]

    def products(weight_ref, owner):
        columns = pl.ds(pl.multiple_of((2 * owner + core) * depth, depth), depth)
        weight = weight_ref[...]
        return (
            jnp.dot(latents_ref[:, columns], weight, preferred_element_type=F32),
            jnp.dot(partner_ref[:, columns], weight, preferred_element_type=F32),
        )

    mine = other = None
    if carried:
        mine, other = carried_mine[...], carried_other[...]
    for weight_ref, (owner_of, here) in zip(weights, slots):
        if here is None:
            add_mine, add_other = products(weight_ref, owner_of(chip))
            mine = add_mine if mine is None else mine + add_mine
            other = add_other if other is None else other + add_other
    mine_ref[...], other_ref[...] = mine, other
    for weight_ref, (owner_of, here) in zip(weights, slots):
        if here is not None:

            @pl.when(here(chip, chips))
            def _():
                add_mine, add_other = products(weight_ref, owner_of(chip))
                mine_ref[...] += add_mine
                other_ref[...] += add_other


def partial_product(latents, partner_latents, weights, slots, carry):
    rows = latents.shape[0]
    depth, width = weights[0].shape
    count = len(weights)
    carry = list(carry)
    return pl.pallas_call(
        functools.partial(partial_body, tuple(slots), bool(carry)),
        out_shape=[shape_of((rows, width), F32)] * 2,
        in_specs=[VMEM] * (2 + count + len(carry)),
        out_specs=[VMEM] * 2,
        cost_estimate=cost(4 * rows * depth * width * count, 4 * rows * depth * count),
        compiler_params=GRANT,
        name="partial_product",
    )(latents, partner_latents, *weights, *carry)


def finish_body(head_size, has_partner, *refs):
    total = refs[0][...]
    if has_partner:
        total = total + refs[1][...]
        refs = refs[1:]
    gains = refs[1][...]
    query_ref, pair_ref = refs[2:]
    query_ref[...] = root_norm(total[:, :head_size], gains[0:1]).astype(BF16)
    keys = root_norm(total[:, head_size : 2 * head_size], gains[1:2])
    pair_ref[:, :head_size] = keys.astype(BF16)
    pair_ref[:, head_size:] = total[:, 2 * head_size :].astype(BF16)


def finish_projection(parts, norm_gains):
    rows, width = parts[0].shape
    head_size = norm_gains.shape[1]
    return pl.pallas_call(
        functools.partial(finish_body, head_size, len(parts) > 1),
        out_shape=[shape_of((rows, head_size), BF16), shape_of((rows, 2 * head_size), BF16)],
        in_specs=[VMEM] * (len(parts) + 1),
        out_specs=[VMEM] * 2,
        cost_estimate=cost(10 * rows * width, 10 * rows * width, 2 * rows),
        compiler_params=GRANT,
        name="finish_projection",
    )(*parts, norm_gains)


def project(latents, input_weight, norm_gains):
    devices = lax.axis_size("grid")
    chips = devices // 2
    if devices % 2 or chips != 4:
        weight = lax.all_gather(input_weight, "grid", axis=0, tiled=True)
        total = jnp.dot(latents, weight, preferred_element_type=F32)
        return finish_projection([total], norm_gains)
    every = range(devices)
    swap = [(at, at ^ 1) for at in every]
    across = [(at, at ^ chips) for at in every]
    up = [(at, at + 2) for at in every if at + 2 < devices]
    down = [(at, at - 2) for at in every if at >= 2]
    outward = [(at, at - 2) for at in (2, 3)] + [
        (at, at + 2) for at in (devices - 4, devices - 3)
    ]
    far = lax.ppermute(input_weight, "grid", across)
    below = lax.ppermute(input_weight, "grid", up)
    above = lax.ppermute(input_weight, "grid", down)
    partner_latents = lax.ppermute(latents, "grid", swap)
    relayed = lax.ppermute(far, "grid", outward)
    half = chips // 2
    carry = partial_product(
        latents,
        partner_latents,
        [input_weight, far],
        [(lambda chip: chip, None), (lambda chip: lax.rem(chip + half, chips), None)],
        (),
    )
    carry = partial_product(
        latents,
        partner_latents,
        [below, above],
        [
            (lambda chip: chip - 1, lambda chip, chips: chip > 0),
            (lambda chip: chip + 1, lambda chip, chips: chip < chips - 1),
        ],
        carry,
    )
    mine, other = partial_product(
        latents,
        partner_latents,
        [relayed],
        [(lambda chip: chips - 1 - chip, lambda chip, chips: (chip == 0) | (chip == chips - 1))],
        carry,
    )
    return finish_projection([mine, lax.ppermute(other, "grid", swap)], norm_gains)


def attend(state, query, keys, values, factor, live=None):
    scores = lax.dot_general(query, keys, (((1,), (1,)), ((), ())), preferred_element_type=F32)
    if live is not None:
        scores = jnp.where(live, scores, -jnp.inf)
    top = scores.max(-1, keepdims=True)
    if state is None:
        weights = jnp.exp2((scores - top) * factor)
        mixed = jnp.dot(weights.astype(BF16), values, preferred_element_type=F32)
        return top, weights.sum(-1, keepdims=True), mixed
    old_top, old_sum, old_mixed = state
    top = jnp.maximum(old_top, top)
    fade = jnp.exp2((old_top - top) * factor)
    weights = jnp.exp2((scores - top) * factor)
    mixed = jnp.dot(weights.astype(BF16), values, preferred_element_type=F32)
    return top, old_sum * fade + weights.sum(-1, keepdims=True), old_mixed * fade + mixed


def outer_height(height):
    return jnp.where(lax.rem(height, 2) == 0, height - 1, height + 1)


def attend_body(slots, with_text, carried, last, factor, *refs):
    place = lax.axis_index("grid")
    times = lax.axis_size("grid") // GRID_H
    time, height = place // GRID_H, lax.rem(place, GRID_H)
    beyond = outer_height(height)
    outer_ok = (beyond >= 0) & (beyond < GRID_H)
    query_ref, refs = refs[0], refs[1:]
    pair_refs, refs = refs[: len(slots)], refs[len(slots) :]
    head_size = query_ref.shape[1]
    query = query_ref[...]
    rows = query.shape[0]
    state = None
    if with_text:
        count_ref, text_ref, gains_ref = refs[:3]
        refs = refs[3:]
    if carried:
        state = refs[0][:, 0:1], refs[1][:, 0:1], refs[2][...]
        refs = refs[3:]
    scratch = refs[-3:]
    outs = refs[:-3]
    if with_text:
        text_keys = root_norm(text_ref[:, :head_size].astype(F32), gains_ref[1:2]).astype(BF16)
        live = lax.broadcasted_iota(jnp.int32, (rows, text_ref.shape[0]), 1) < count_ref[0]
        state = attend(state, query, text_keys, text_ref[:, head_size:], factor, live)
    gates = []
    for by, outer in slots:
        gate = None
        if by is not None:
            gate = (time - by >= 0) & (time - by < times)
        if outer:
            gate = outer_ok if gate is None else gate & outer_ok
        gates.append(gate)
    for pair_ref, gate in zip(pair_refs, gates):
        if gate is None:
            pair = pair_ref[...]
            state = attend(state, query, pair[:, :head_size], pair[:, head_size:], factor)
    for pair_ref, gate in zip(pair_refs, gates):
        if gate is not None:
            scratch[0][...], scratch[1][...], scratch[2][...] = state

            @pl.when(gate)
            def _():
                pair = pair_ref[...]
                before = scratch[0][...], scratch[1][...], scratch[2][...]
                after = attend(before, query, pair[:, :head_size], pair[:, head_size:], factor)
                scratch[0][...], scratch[1][...], scratch[2][...] = after

            state = scratch[0][...], scratch[1][...], scratch[2][...]
    top, total, mixed = state
    if last:
        outs[0][...] = (mixed / total).astype(BF16)
    else:
        outs[0][...] = jnp.broadcast_to(top, outs[0].shape)
        outs[1][...] = jnp.broadcast_to(total, outs[1].shape)
        outs[2][...] = mixed


def attention_step(query, pairs, slots, text=(), carry=(), last=False):
    rows, head_size = query.shape
    factor = head_size ** (-0.5) * LOG2E
    text, carry = list(text), list(carry)
    plane = shape_of((rows, head_size), F32)
    columns = sum(pair.shape[0] for pair in pairs)
    return pl.pallas_call(
        functools.partial(attend_body, tuple(slots), bool(text), bool(carry), last, factor),
        out_shape=shape_of((rows, head_size), BF16) if last else [plane] * 3,
        in_specs=[VMEM] * (1 + len(pairs))
        + ([SMEM, VMEM, VMEM] if text else [])
        + [VMEM] * len(carry),
        out_specs=VMEM if last else [VMEM] * 3,
        scratch_shapes=[
            pltpu.VMEM((rows, 1), F32),
            pltpu.VMEM((rows, 1), F32),
            pltpu.VMEM((rows, head_size), F32),
        ],
        cost_estimate=cost(4 * rows * columns * head_size, 4 * columns * head_size, rows * columns),
        compiler_params=GRANT,
        name="attention_step",
    )(query, *pairs, *text, *carry)


def attention_rows(query, pair, text_pairs, norm_gains, text_count):
    devices = lax.axis_size("grid")
    times = devices // GRID_H
    swap = [(at, at ^ 1) for at in range(devices)]
    outer = []
    for at in range(devices):
        row = at % GRID_H
        beyond = row - 1 if row % 2 == 0 else row + 1
        if 0 <= beyond < GRID_H:
            outer.append((at, at - row + beyond))

    def later(pairs, by):
        return [(at, to + by * GRID_H) for at, to in pairs if 0 <= to + by * GRID_H < devices]

    same = [(at, at) for at in range(devices)]
    if times == 2:
        half = devices // 2
        plans = [(None, [(at, at ^ half) for at in range(devices)], [(at, to ^ half) for at, to in outer])]
    elif times > 2:
        plans = [(by, later(same, by), later(outer, by)) for by in (1, -1)]
    else:
        plans = []
    far = [lax.ppermute(pair, "grid", along) for _, along, _ in plans]
    partner = lax.ppermute(pair, "grid", swap)
    near_outer = lax.ppermute(pair, "grid", outer)
    far_outer = [lax.ppermute(pair, "grid", over) for _, _, over in plans]
    text = (text_count, text_pairs, norm_gains)
    carry = attention_step(query, [pair], [(None, False)], text=text)
    carry = attention_step(
        query, [partner, near_outer], [(None, False), (None, True)], carry=carry, last=not plans
    )
    for at, (by, _, _) in enumerate(plans):
        carry = attention_step(
            query, [far[at], far_outer[at]], [(by, False), (by, True)], carry=carry
        )
        carry = attention_step(
            query,
            [lax.ppermute(far[at], "grid", swap)],
            [(by, False)],
            carry=carry,
            last=at == len(plans) - 1,
        )
    return carry


def output_body(groups, *refs):
    attention, refs = refs[:groups], refs[groups:]
    mine_ref, other_ref, out_ref, held, joined = refs
    place, group = lax.axis_index("grid"), lax.axis_index("tp")
    chip, core = place // 2, lax.rem(place, 2)
    depth, width = mine_ref.shape[0] // groups, mine_ref.shape[1]
    for at in range(groups):
        held[at] = attention[at][...]
    for turn in range(groups):
        source = lax.rem(chip + groups - turn, groups)
        joined[:, turn * depth : (turn + 1) * depth] = held[group ^ source]
    rows = joined[...]
    mine = jnp.dot(rows, mine_ref[...], preferred_element_type=F32).astype(BF16)
    other = jnp.dot(rows, other_ref[...], preferred_element_type=F32).astype(BF16)

    @pl.when(core == 0)
    def _():
        out_ref[:, :width] = mine
        out_ref[:, width:] = other

    @pl.when(core != 0)
    def _():
        out_ref[:, :width] = other
        out_ref[:, width:] = mine


def output_product(attention, mine, other):
    groups = len(attention)
    rows, depth = attention[0].shape
    width = mine.shape[1]
    return pl.pallas_call(
        functools.partial(output_body, groups),
        out_shape=shape_of((rows, 2 * width), BF16),
        in_specs=[VMEM] * (groups + 2),
        out_specs=VMEM,
        scratch_shapes=[
            pltpu.VMEM((groups, rows, depth), BF16),
            pltpu.VMEM((rows, groups * depth), BF16),
        ],
        cost_estimate=cost(
            4 * rows * depth * groups * width, 4 * depth * groups * width + 4 * rows * width
        ),
        compiler_params=GRANT,
        name="output_product",
    )(*attention, mine, other)


def direct_output(devices, groups):
    return devices == 2 * groups and groups == 4


def send_output_weight(output_weight):
    groups = lax.axis_size("tp")

    def flat(chip, core, group):
        return (2 * chip + core) * groups + group

    pieces = []
    for turn in range(groups):
        pairs = [
            (flat(chip, core, group), flat((group + turn) % groups, core, chip))
            for chip in range(groups)
            for core in range(2)
            for group in range(groups)
        ]
        pieces.append(lax.ppermute(output_weight, ("grid", "tp"), pairs))
    return pieces


def local(latents, input_weight, norm_gains, text_pairs, text_count, output_weight):
    devices, groups = lax.axis_size("grid"), lax.axis_size("tp")
    direct = direct_output(devices, groups)
    if direct:
        pieces = send_output_weight(output_weight)
    query, pair = project(latents, input_weight, norm_gains)
    attention = attention_rows(query, pair, text_pairs, norm_gains, text_count)
    if not direct:
        weight = lax.all_gather(output_weight, "grid", axis=1, tiled=True)
        term = jnp.dot(attention, weight, preferred_element_type=F32)
        return lax.psum_scatter(term.astype(BF16), "tp", scatter_dimension=1, tiled=True)
    mine = jnp.concatenate(pieces, axis=0)
    other = lax.ppermute(mine, "grid", [(at, at ^ 1) for at in range(devices)])
    gathered = [attention] + [
        lax.ppermute(attention, "tp", [(at, at ^ by) for at in range(groups)])
        for by in range(1, groups)
    ]
    return output_product(gathered, mine, other)


def solution(mesh):
    placed = (P("grid", None), P("grid", "tp"), P(), P(None, "tp"), P(), P("tp", "grid"))
    return jax.shard_map(
        local, mesh=mesh, in_specs=placed, out_specs=P("grid", "tp"), check_vma=False
    )
```

```python
import functools

import jax
import jax.numpy as jnp
import numpy as np
from jax import lax
from jax.experimental import pallas as pl
from jax.experimental.pallas import tpu as pltpu
from jax.sharding import PartitionSpec as P


GRID_H = 4
LOG2E = float(np.log2(np.e))

epsilon = 1e-06


F32 = jnp.float32
BF16 = jnp.bfloat16
VMEM = pl.BlockSpec(memory_space=pltpu.VMEM)
SMEM = pl.BlockSpec(memory_space=pltpu.SMEM)
GRANT = pltpu.CompilerParams(vmem_limit_bytes=16 * 1024 * 1024)


def shape_of(shape, dtype):
    return jax.ShapeDtypeStruct(shape, dtype)


def cost(flops, bytes_accessed, transcendentals=0):
    return pl.CostEstimate(
        flops=int(flops), bytes_accessed=int(bytes_accessed), transcendentals=int(transcendentals)
    )


def root_norm(values, gain):
    return values * lax.rsqrt(jnp.mean(values * values, axis=-1, keepdims=True) + epsilon) * gain


def partial_body(slots, carried, latents_ref, partner_ref, *refs):
    chips = lax.axis_size("grid") // 2
    place = lax.axis_index("grid")
    chip, core = place // 2, lax.rem(place, 2)
    weights, refs = refs[: len(slots)], refs[len(slots) :]
    if carried:
        carried_mine, carried_other = refs[:2]
        refs = refs[2:]
    mine_ref, other_ref = refs
    depth = weights[0].shape[0]

    def products(weight_ref, owner):
        columns = pl.ds(pl.multiple_of((2 * owner + core) * depth, depth), depth)
        weight = weight_ref[...]
        return (
            jnp.dot(latents_ref[:, columns], weight, preferred_element_type=F32),
            jnp.dot(partner_ref[:, columns], weight, preferred_element_type=F32),
        )

    mine = other = None
    if carried:
        mine, other = carried_mine[...], carried_other[...]
    for weight_ref, (owner_of, here) in zip(weights, slots):
        if here is None:
            add_mine, add_other = products(weight_ref, owner_of(chip))
            mine = add_mine if mine is None else mine + add_mine
            other = add_other if other is None else other + add_other
    mine_ref[...], other_ref[...] = mine, other
    for weight_ref, (owner_of, here) in zip(weights, slots):
        if here is not None:

            @pl.when(here(chip, chips))
            def _():
                add_mine, add_other = products(weight_ref, owner_of(chip))
                mine_ref[...] += add_mine
                other_ref[...] += add_other


def partial_product(latents, partner_latents, weights, slots, carry):
    rows = latents.shape[0]
    depth, width = weights[0].shape
    count = len(weights)
    carry = list(carry)
    return pl.pallas_call(
        functools.partial(partial_body, tuple(slots), bool(carry)),
        out_shape=[shape_of((rows, width), F32)] * 2,
        in_specs=[VMEM] * (2 + count + len(carry)),
        out_specs=[VMEM] * 2,
        cost_estimate=cost(4 * rows * depth * width * count, 4 * rows * depth * count),
        compiler_params=GRANT,
        name="partial_product",
    )(latents, partner_latents, *weights, *carry)


def keys_body(head_size, mine_ref, other_ref, gains_ref, pair_ref):
    total = mine_ref[...] + other_ref[...]
    keys = root_norm(total[:, :head_size], gains_ref[1:2])
    pair_ref[:, :head_size] = keys.astype(BF16)
    pair_ref[:, head_size:] = total[:, head_size:].astype(BF16)


def query_body(mine_ref, other_ref, gains_ref, query_ref):
    query_ref[...] = root_norm(mine_ref[...] + other_ref[...], gains_ref[0:1]).astype(BF16)


def finish(body, mine, other, norm_gains):
    rows, width = mine.shape
    return pl.pallas_call(
        body,
        out_shape=shape_of((rows, width), BF16),
        in_specs=[VMEM] * 3,
        out_specs=VMEM,
        cost_estimate=cost(10 * rows * width, 10 * rows * width, rows),
        compiler_params=GRANT,
    )(mine, other, norm_gains)


def project(latents, input_weight, norm_gains):
    devices = lax.axis_size("grid")
    chips = devices // 2
    head_size = norm_gains.shape[1]
    finish_keys = functools.partial(keys_body, head_size)
    if devices % 2 or chips != 4:
        weight = lax.all_gather(input_weight, "grid", axis=0, tiled=True)
        total = jnp.dot(latents, weight, preferred_element_type=F32)
        zero = jnp.zeros_like(total)
        query = finish(query_body, total[:, :head_size], zero[:, :head_size], norm_gains)
        pair = finish(finish_keys, total[:, head_size:], zero[:, head_size:], norm_gains)
        return query, pair
    every = range(devices)
    swap = [(at, at ^ 1) for at in every]
    across = [(at, at ^ chips) for at in every]
    up = [(at, at + 2) for at in every if at + 2 < devices]
    down = [(at, at - 2) for at in every if at >= 2]
    outward = [(at, at - 2) for at in (2, 3)] + [
        (at, at + 2) for at in (devices - 4, devices - 3)
    ]
    half = chips // 2
    pair_weight, query_weight = input_weight[:, head_size:], input_weight[:, :head_size]
    far = lax.ppermute(pair_weight, "grid", across)
    below = lax.ppermute(pair_weight, "grid", up)
    above = lax.ppermute(pair_weight, "grid", down)
    partner_latents = lax.ppermute(latents, "grid", swap)
    relayed = lax.ppermute(far, "grid", outward)
    query_shards = [query_weight] + [
        lax.ppermute(query_weight, "grid", [(at, (at + 2 * turn) % devices) for at in every])
        for turn in range(1, chips)
    ]
    carry = partial_product(
        latents,
        partner_latents,
        [pair_weight, far],
        [(lambda chip: chip, None), (lambda chip: lax.rem(chip + half, chips), None)],
        (),
    )
    carry = partial_product(
        latents,
        partner_latents,
        [below, above],
        [
            (lambda chip: chip - 1, lambda chip, chips: chip > 0),
            (lambda chip: chip + 1, lambda chip, chips: chip < chips - 1),
        ],
        carry,
    )
    mine, other = partial_product(
        latents,
        partner_latents,
        [relayed],
        [(lambda chip: chips - 1 - chip, lambda chip, chips: (chip == 0) | (chip == chips - 1))],
        carry,
    )
    pair = finish(finish_keys, mine, lax.ppermute(other, "grid", swap), norm_gains)
    mine, other = partial_product(
        latents,
        partner_latents,
        query_shards,
        [
            (lambda chip, turn=turn: lax.rem(chip + chips - turn, chips), None)
            for turn in range(chips)
        ],
        (),
    )
    query = finish(query_body, mine, lax.ppermute(other, "grid", swap), norm_gains)
    return query, pair


def attend(state, query, keys, values, factor, live=None):
    scores = lax.dot_general(query, keys, (((1,), (1,)), ((), ())), preferred_element_type=F32)
    if live is not None:
        scores = jnp.where(live, scores, -jnp.inf)
    top = scores.max(-1, keepdims=True)
    if state is None:
        weights = jnp.exp2((scores - top) * factor)
        mixed = jnp.dot(weights.astype(BF16), values, preferred_element_type=F32)
        return top, weights.sum(-1, keepdims=True), mixed
    old_top, old_sum, old_mixed = state
    top = jnp.maximum(old_top, top)
    fade = jnp.exp2((old_top - top) * factor)
    weights = jnp.exp2((scores - top) * factor)
    mixed = jnp.dot(weights.astype(BF16), values, preferred_element_type=F32)
    return top, old_sum * fade + weights.sum(-1, keepdims=True), old_mixed * fade + mixed


def outer_height(height):
    return jnp.where(lax.rem(height, 2) == 0, height - 1, height + 1)


def attend_body(slots, with_text, carried, last, factor, *refs):
    place = lax.axis_index("grid")
    times = lax.axis_size("grid") // GRID_H
    time, height = place // GRID_H, lax.rem(place, GRID_H)
    beyond = outer_height(height)
    outer_ok = (beyond >= 0) & (beyond < GRID_H)
    query_ref, refs = refs[0], refs[1:]
    pair_refs, refs = refs[: len(slots)], refs[len(slots) :]
    head_size = query_ref.shape[1]
    query = query_ref[...]
    rows = query.shape[0]
    state = None
    if with_text:
        count_ref, text_ref, gains_ref = refs[:3]
        refs = refs[3:]
    if carried:
        state = refs[0][:, 0:1], refs[1][:, 0:1], refs[2][...]
        refs = refs[3:]
    scratch = refs[-3:]
    outs = refs[:-3]
    if with_text:
        text_keys = root_norm(text_ref[:, :head_size].astype(F32), gains_ref[1:2]).astype(BF16)
        live = lax.broadcasted_iota(jnp.int32, (rows, text_ref.shape[0]), 1) < count_ref[0]
        state = attend(state, query, text_keys, text_ref[:, head_size:], factor, live)
    gates = []
    for by, outer in slots:
        gate = None
        if by is not None:
            gate = (time - by >= 0) & (time - by < times)
        if outer:
            gate = outer_ok if gate is None else gate & outer_ok
        gates.append(gate)
    for pair_ref, gate in zip(pair_refs, gates):
        if gate is None:
            pair = pair_ref[...]
            state = attend(state, query, pair[:, :head_size], pair[:, head_size:], factor)
    for pair_ref, gate in zip(pair_refs, gates):
        if gate is not None:
            scratch[0][...], scratch[1][...], scratch[2][...] = state

            @pl.when(gate)
            def _():
                pair = pair_ref[...]
                before = scratch[0][...], scratch[1][...], scratch[2][...]
                after = attend(before, query, pair[:, :head_size], pair[:, head_size:], factor)
                scratch[0][...], scratch[1][...], scratch[2][...] = after

            state = scratch[0][...], scratch[1][...], scratch[2][...]
    top, total, mixed = state
    if last:
        outs[0][...] = (mixed / total).astype(BF16)
    else:
        outs[0][...] = jnp.broadcast_to(top, outs[0].shape)
        outs[1][...] = jnp.broadcast_to(total, outs[1].shape)
        outs[2][...] = mixed


def attention_step(query, pairs, slots, text=(), carry=(), last=False):
    rows, head_size = query.shape
    factor = head_size ** (-0.5) * LOG2E
    text, carry = list(text), list(carry)
    plane = shape_of((rows, head_size), F32)
    columns = sum(pair.shape[0] for pair in pairs)
    return pl.pallas_call(
        functools.partial(attend_body, tuple(slots), bool(text), bool(carry), last, factor),
        out_shape=shape_of((rows, head_size), BF16) if last else [plane] * 3,
        in_specs=[VMEM] * (1 + len(pairs))
        + ([SMEM, VMEM, VMEM] if text else [])
        + [VMEM] * len(carry),
        out_specs=VMEM if last else [VMEM] * 3,
        scratch_shapes=[
            pltpu.VMEM((rows, 1), F32),
            pltpu.VMEM((rows, 1), F32),
            pltpu.VMEM((rows, head_size), F32),
        ],
        cost_estimate=cost(4 * rows * columns * head_size, 4 * columns * head_size, rows * columns),
        compiler_params=GRANT,
        name="attention_step",
    )(query, *pairs, *text, *carry)


def attention_rows(query, pair, text_pairs, norm_gains, text_count):
    devices = lax.axis_size("grid")
    times = devices // GRID_H
    swap = [(at, at ^ 1) for at in range(devices)]
    outer = []
    for at in range(devices):
        row = at % GRID_H
        beyond = row - 1 if row % 2 == 0 else row + 1
        if 0 <= beyond < GRID_H:
            outer.append((at, at - row + beyond))

    def later(pairs, by):
        return [(at, to + by * GRID_H) for at, to in pairs if 0 <= to + by * GRID_H < devices]

    same = [(at, at) for at in range(devices)]
    if times == 2:
        half = devices // 2
        plans = [(None, [(at, at ^ half) for at in range(devices)], [(at, to ^ half) for at, to in outer])]
    elif times > 2:
        plans = [(by, later(same, by), later(outer, by)) for by in (1, -1)]
    else:
        plans = []

    def filled(pairs):
        sources, targets = {at for at, _ in pairs}, {to for _, to in pairs}
        return pairs + [(at, at) for at in range(devices) if at not in sources and at not in targets]

    far = [lax.ppermute(pair, "grid", along) for _, along, _ in plans]
    partner = lax.ppermute(pair, "grid", swap)
    near_outer = lax.ppermute(pair, "grid", filled(outer))
    far_outer = [lax.ppermute(pair, "grid", filled(over)) for _, _, over in plans]
    text = (text_count, text_pairs, norm_gains)
    carry = attention_step(query, [pair, partner], [(None, False), (None, False)], text=text)
    carry = attention_step(query, [near_outer], [(None, True)], carry=carry, last=not plans)
    for at, (by, _, _) in enumerate(plans):
        far_partner = lax.ppermute(far[at], "grid", swap)
        carry = attention_step(query, [far[at]], [(by, False)], carry=carry)
        carry = attention_step(
            query,
            [far_partner, far_outer[at]],
            [(by, False), (by, True)],
            carry=carry,
            last=at == len(plans) - 1,
        )
    return carry


def output_body(groups, *refs):
    attention, refs = refs[:groups], refs[groups:]
    mine_ref, other_ref, out_ref, held, joined = refs
    place, group = lax.axis_index("grid"), lax.axis_index("tp")
    chip, core = place // 2, lax.rem(place, 2)
    depth, width = mine_ref.shape[0] // groups, mine_ref.shape[1]
    for at in range(groups):
        held[at] = attention[at][...]
    for turn in range(groups):
        source = lax.rem(chip + groups - turn, groups)
        joined[:, turn * depth : (turn + 1) * depth] = held[group ^ source]
    rows = joined[...]
    mine = jnp.dot(rows, mine_ref[...], preferred_element_type=F32).astype(BF16)
    other = jnp.dot(rows, other_ref[...], preferred_element_type=F32).astype(BF16)

    @pl.when(core == 0)
    def _():
        out_ref[:, :width] = mine
        out_ref[:, width:] = other

    @pl.when(core != 0)
    def _():
        out_ref[:, :width] = other
        out_ref[:, width:] = mine


def output_product(attention, mine, other):
    groups = len(attention)
    rows, depth = attention[0].shape
    width = mine.shape[1]
    return pl.pallas_call(
        functools.partial(output_body, groups),
        out_shape=shape_of((rows, 2 * width), BF16),
        in_specs=[VMEM] * (groups + 2),
        out_specs=VMEM,
        scratch_shapes=[
            pltpu.VMEM((groups, rows, depth), BF16),
            pltpu.VMEM((rows, groups * depth), BF16),
        ],
        cost_estimate=cost(
            4 * rows * depth * groups * width, 4 * depth * groups * width + 4 * rows * width
        ),
        compiler_params=GRANT,
        name="output_product",
    )(*attention, mine, other)


def direct_output(devices, groups):
    return devices == 2 * groups and groups == 4


def send_output_weight(output_weight):
    groups = lax.axis_size("tp")

    def flat(chip, core, group):
        return (2 * chip + core) * groups + group

    pieces = []
    for turn in range(groups):
        pairs = [
            (flat(chip, core, group), flat((group + turn) % groups, core, chip))
            for chip in range(groups)
            for core in range(2)
            for group in range(groups)
        ]
        pieces.append(lax.ppermute(output_weight, ("grid", "tp"), pairs))
    return pieces


def local(latents, input_weight, norm_gains, text_pairs, text_count, output_weight):
    devices, groups = lax.axis_size("grid"), lax.axis_size("tp")
    direct = direct_output(devices, groups)
    if direct:
        pieces = send_output_weight(output_weight)
    query, pair = project(latents, input_weight, norm_gains)
    attention = attention_rows(query, pair, text_pairs, norm_gains, text_count)
    if not direct:
        weight = lax.all_gather(output_weight, "grid", axis=1, tiled=True)
        term = jnp.dot(attention, weight, preferred_element_type=F32)
        return lax.psum_scatter(term.astype(BF16), "tp", scatter_dimension=1, tiled=True)
    mine = jnp.concatenate(pieces, axis=0)
    other = lax.ppermute(mine, "grid", [(at, at ^ 1) for at in range(devices)])
    gathered = [attention] + [
        lax.ppermute(attention, "tp", [(at, at ^ by) for at in range(groups)])
        for by in range(1, groups)
    ]
    return output_product(gathered, mine, other)


def solution(mesh):
    placed = (P("grid", None), P("grid", "tp"), P(), P(None, "tp"), P(), P("tp", "grid"))
    return jax.shard_map(
        local, mesh=mesh, in_specs=placed, out_specs=P("grid", "tp"), check_vma=False
    )
```

```python
import functools

import jax
import jax.numpy as jnp
import numpy as np
from jax import lax
from jax.experimental import pallas as pl
from jax.experimental.pallas import tpu as pltpu
from jax.sharding import PartitionSpec as P


GRID_H = 4
LOG2E = float(np.log2(np.e))

epsilon = 1e-06


F32 = jnp.float32
BF16 = jnp.bfloat16
VMEM = pl.BlockSpec(memory_space=pltpu.VMEM)
SMEM = pl.BlockSpec(memory_space=pltpu.SMEM)
GRANT = pltpu.CompilerParams(vmem_limit_bytes=16 * 1024 * 1024)


def shape_of(shape, dtype):
    return jax.ShapeDtypeStruct(shape, dtype)


def cost(flops, bytes_accessed, transcendentals=0):
    return pl.CostEstimate(
        flops=int(flops), bytes_accessed=int(bytes_accessed), transcendentals=int(transcendentals)
    )


def root_norm(values, gain):
    return values * lax.rsqrt(jnp.mean(values * values, axis=-1, keepdims=True) + epsilon) * gain


def partial_body(slots, carried, latents_ref, partner_ref, *refs):
    chips = lax.axis_size("grid") // 2
    place = lax.axis_index("grid")
    chip, core = place // 2, lax.rem(place, 2)
    weights, refs = refs[: len(slots)], refs[len(slots) :]
    if carried:
        carried_mine, carried_other = refs[:2]
        refs = refs[2:]
    mine_ref, other_ref = refs
    depth = weights[0].shape[0]

    def products(weight_ref, owner):
        columns = pl.ds(pl.multiple_of((2 * owner + core) * depth, depth), depth)
        weight = weight_ref[...]
        return (
            jnp.dot(latents_ref[:, columns], weight, preferred_element_type=F32),
            jnp.dot(partner_ref[:, columns], weight, preferred_element_type=F32),
        )

    mine = other = None
    if carried:
        mine, other = carried_mine[...], carried_other[...]
    for weight_ref, (owner_of, here) in zip(weights, slots):
        if here is None:
            add_mine, add_other = products(weight_ref, owner_of(chip))
            mine = add_mine if mine is None else mine + add_mine
            other = add_other if other is None else other + add_other
    mine_ref[...], other_ref[...] = mine, other
    for weight_ref, (owner_of, here) in zip(weights, slots):
        if here is not None:

            @pl.when(here(chip, chips))
            def _():
                add_mine, add_other = products(weight_ref, owner_of(chip))
                mine_ref[...] += add_mine
                other_ref[...] += add_other


def partial_product(latents, partner_latents, weights, slots, carry):
    rows = latents.shape[0]
    depth, width = weights[0].shape
    count = len(weights)
    carry = list(carry)
    return pl.pallas_call(
        functools.partial(partial_body, tuple(slots), bool(carry)),
        out_shape=[shape_of((rows, width), F32)] * 2,
        in_specs=[VMEM] * (2 + count + len(carry)),
        out_specs=[VMEM] * 2,
        cost_estimate=cost(4 * rows * depth * width * count, 4 * rows * depth * count),
        compiler_params=GRANT,
        name="partial_product",
    )(latents, partner_latents, *weights, *carry)


def keys_body(head_size, mine_ref, other_ref, gains_ref, pair_ref):
    total = mine_ref[...] + other_ref[...]
    keys = root_norm(total[:, :head_size], gains_ref[1:2])
    pair_ref[:, :head_size] = keys.astype(BF16)
    pair_ref[:, head_size:] = total[:, head_size:].astype(BF16)


def query_body(mine_ref, other_ref, gains_ref, query_ref):
    query_ref[...] = root_norm(mine_ref[...] + other_ref[...], gains_ref[0:1]).astype(BF16)


def finish(body, mine, other, norm_gains):
    rows, width = mine.shape
    return pl.pallas_call(
        body,
        out_shape=shape_of((rows, width), BF16),
        in_specs=[VMEM] * 3,
        out_specs=VMEM,
        cost_estimate=cost(10 * rows * width, 10 * rows * width, rows),
        compiler_params=GRANT,
    )(mine, other, norm_gains)


def filled(pairs, devices):
    sources, targets = {at for at, _ in pairs}, {to for _, to in pairs}
    return pairs + [(at, at) for at in range(devices) if at not in sources | targets]


def project(latents, input_weight, norm_gains):
    devices = lax.axis_size("grid")
    chips = devices // 2
    head_size = norm_gains.shape[1]
    finish_keys = functools.partial(keys_body, head_size)
    if devices % 2 or chips != 4:
        weight = lax.all_gather(input_weight, "grid", axis=0, tiled=True)
        total = jnp.dot(latents, weight, preferred_element_type=F32)
        zero = jnp.zeros_like(total)
        query = finish(query_body, total[:, :head_size], zero[:, :head_size], norm_gains)
        pair = finish(finish_keys, total[:, head_size:], zero[:, head_size:], norm_gains)
        return query, pair
    every = range(devices)
    swap = [(at, at ^ 1) for at in every]
    across = [(at, at ^ chips) for at in every]
    up = [(at, at + 2) for at in every if at + 2 < devices]
    down = [(at, at - 2) for at in every if at >= 2]
    outward = [(at, at - 2) for at in (2, 3)] + [
        (at, at + 2) for at in (devices - 4, devices - 3)
    ]
    half = chips // 2
    pair_weight, query_weight = input_weight[:, head_size:], input_weight[:, :head_size]
    far = lax.ppermute(pair_weight, "grid", across)
    below = lax.ppermute(pair_weight, "grid", up)
    above = lax.ppermute(pair_weight, "grid", down)
    partner_latents = lax.ppermute(latents, "grid", swap)
    relayed = lax.ppermute(far, "grid", outward)
    query_shards = [query_weight] + [
        lax.ppermute(query_weight, "grid", [(at, (at + 2 * turn) % devices) for at in every])
        for turn in range(1, chips)
    ]
    carry = partial_product(
        latents,
        partner_latents,
        [pair_weight, far],
        [(lambda chip: chip, None), (lambda chip: lax.rem(chip + half, chips), None)],
        (),
    )
    carry = partial_product(
        latents,
        partner_latents,
        [below, above],
        [
            (lambda chip: chip - 1, lambda chip, chips: chip > 0),
            (lambda chip: chip + 1, lambda chip, chips: chip < chips - 1),
        ],
        carry,
    )
    mine, other = partial_product(
        latents,
        partner_latents,
        [relayed],
        [(lambda chip: chips - 1 - chip, lambda chip, chips: (chip == 0) | (chip == chips - 1))],
        carry,
    )
    pair = finish(finish_keys, mine, lax.ppermute(other, "grid", swap), norm_gains)
    mine, other = partial_product(
        latents,
        partner_latents,
        query_shards,
        [
            (lambda chip, turn=turn: lax.rem(chip + chips - turn, chips), None)
            for turn in range(chips)
        ],
        (),
    )
    query = finish(query_body, mine, lax.ppermute(other, "grid", swap), norm_gains)
    return query, pair


def attend(state, query, tiles, factor):
    rows, head_size = query.shape
    scores = []
    for keys, _, live in tiles:
        score = lax.dot_general(query, keys, (((1,), (1,)), ((), ())), preferred_element_type=F32)
        for at in range(0, keys.shape[0], head_size):
            part = score[:, at : at + head_size]
            if live is not None:
                part = jnp.where(live[:, at : at + head_size], part, -jnp.inf)
            scores.append(part)
    top = functools.reduce(jnp.maximum, scores).max(-1, keepdims=True)
    top = jnp.broadcast_to(top, (rows, head_size)) * factor
    if state is not None:
        top = jnp.maximum(state[0], top)
    mixed = None
    at = 0
    for keys, values, _ in tiles:
        count = keys.shape[0] // head_size
        weights = [jnp.exp2(part * factor - top).astype(BF16) for part in scores[at : at + count]]
        at += count
        wide = jnp.concatenate([values, jnp.ones_like(values)], axis=1)
        add = jnp.dot(jnp.concatenate(weights, axis=1), wide, preferred_element_type=F32)
        mixed = add if mixed is None else mixed + add
    total, mixed = mixed[:, head_size:], mixed[:, :head_size]
    if state is not None:
        fade = jnp.exp2(state[0] - top)
        total, mixed = state[1] * fade + total, state[2] * fade + mixed
    return top, total, mixed


def outer_height(height):
    return jnp.where(lax.rem(height, 2) == 0, height - 1, height + 1)


def attend_body(slots, with_text, carried, last, factor, *refs):
    place = lax.axis_index("grid")
    times = lax.axis_size("grid") // GRID_H
    time, height = place // GRID_H, lax.rem(place, GRID_H)
    beyond = outer_height(height)
    outer_ok = (beyond >= 0) & (beyond < GRID_H)
    query_ref, refs = refs[0], refs[1:]
    pair_refs, refs = refs[: len(slots)], refs[len(slots) :]
    head_size = query_ref.shape[1]
    rows = query_ref.shape[0]
    if with_text:
        count_ref, text_ref, gains_ref = refs[:3]
        refs = refs[3:]
    if carried:
        carry, refs = refs[:3], refs[3:]
    held = refs[1:] if last else refs
    out_ref = refs[0]

    def before():
        return tuple(ref[...] for ref in carry) if carried else None

    def tiles_of(which):
        return [
            (pair_refs[at][:, :head_size], pair_refs[at][:, head_size:], None) for at in which
        ]

    def keep(state):
        held[0][...], held[1][...], held[2][...] = state

    def finish(state):
        if last:
            out_ref[...] = (state[2] / state[1]).astype(BF16)
        else:
            keep(state)

    always = [at for at, (by, outer) in enumerate(slots) if by is None and not outer]
    sometimes = [at for at in range(len(slots)) if at not in always]
    if all(slots[at][0] is None for at in sometimes):
        if with_text:
            text_keys = root_norm(text_ref[:, :head_size].astype(F32), gains_ref[1:2]).astype(BF16)
            live = lax.broadcasted_iota(jnp.int32, (rows, text_ref.shape[0]), 1) < count_ref[0]
            extra = [(text_keys, text_ref[:, head_size:], live)]
        else:
            extra = []
        if not sometimes:
            finish(attend(before(), query_ref[...], extra + tiles_of(always), factor))
            return

        @pl.when(outer_ok)
        def _():
            both = extra + tiles_of(always + sometimes)
            finish(attend(before(), query_ref[...], both, factor))

        @pl.when(jnp.logical_not(outer_ok))
        def _():
            some = extra + tiles_of(always)
            finish(attend(before(), query_ref[...], some, factor) if some else before())

        return
    keep(before())
    for at in range(len(slots)):
        by, outer = slots[at]
        gate = (time - by >= 0) & (time - by < times)
        gate = gate & outer_ok if outer else gate

        @pl.when(gate)
        def _():
            state = held[0][...], held[1][...], held[2][...]
            keep(attend(state, query_ref[...], tiles_of([at]), factor))

    if last:
        finish((held[0][...], held[1][...], held[2][...]))


def attention_step(query, pairs, slots, text=(), carry=(), last=False):
    rows, head_size = query.shape
    factor = head_size ** (-0.5) * LOG2E
    text, carry = list(text), list(carry)
    plane = shape_of((rows, head_size), F32)
    columns = sum(pair.shape[0] for pair in pairs)
    return pl.pallas_call(
        functools.partial(attend_body, tuple(slots), bool(text), bool(carry), last, factor),
        out_shape=shape_of((rows, head_size), BF16) if last else [plane] * 3,
        in_specs=[VMEM] * (1 + len(pairs))
        + ([SMEM, VMEM, VMEM] if text else [])
        + [VMEM] * len(carry),
        out_specs=VMEM if last else [VMEM] * 3,
        scratch_shapes=[pltpu.VMEM((rows, head_size), F32)] * 3 if last else [],
        cost_estimate=cost(4 * rows * columns * head_size, 4 * columns * head_size, rows * columns),
        compiler_params=GRANT,
        name="attention_step",
    )(query, *pairs, *text, *carry)


def attention_rows(query, pair, text_pairs, norm_gains, text_count):
    devices = lax.axis_size("grid")
    times = devices // GRID_H
    swap = [(at, at ^ 1) for at in range(devices)]
    outer = []
    for at in range(devices):
        row = at % GRID_H
        beyond = row - 1 if row % 2 == 0 else row + 1
        if 0 <= beyond < GRID_H:
            outer.append((at, at - row + beyond))

    def later(pairs, by):
        return [(at, to + by * GRID_H) for at, to in pairs if 0 <= to + by * GRID_H < devices]

    same = [(at, at) for at in range(devices)]
    if times == 2:
        half = devices // 2
        plans = [(None, [(at, at ^ half) for at in range(devices)], [(at, to ^ half) for at, to in outer])]
    elif times > 2:
        plans = [(by, later(same, by), later(outer, by)) for by in (1, -1)]
    else:
        plans = []
    far = [lax.ppermute(pair, "grid", along) for _, along, _ in plans]
    partner = lax.ppermute(pair, "grid", swap)
    near_outer = lax.ppermute(pair, "grid", filled(outer, devices))
    far_outer = [lax.ppermute(pair, "grid", filled(over, devices)) for _, _, over in plans]
    text = (text_count, text_pairs, norm_gains)
    carry = attention_step(query, [pair, partner], [(None, False), (None, False)], text=text)
    if not plans:
        return attention_step(query, [near_outer], [(None, True)], carry=carry, last=True)
    for at, (by, _, _) in enumerate(plans):
        far_partner = lax.ppermute(far[at], "grid", swap)
        near, near_slots = ([near_outer], [(None, True)]) if by is None else ([], [])
        if by is not None and at == 0:
            carry = attention_step(query, [near_outer], [(None, True)], carry=carry)
        carry = attention_step(query, [far[at], *near], [(by, False), *near_slots], carry=carry)
        carry = attention_step(
            query,
            [far_partner, far_outer[at]],
            [(by, False), (by, True)],
            carry=carry,
            last=at == len(plans) - 1,
        )
    return carry


def output_body(groups, *refs):
    attention, refs = refs[:groups], refs[groups:]
    mine_ref, other_ref, out_ref, held, joined = refs
    place, group = lax.axis_index("grid"), lax.axis_index("tp")
    chip, core = place // 2, lax.rem(place, 2)
    depth, width = mine_ref.shape[0] // groups, mine_ref.shape[1]
    for at in range(groups):
        held[at] = attention[at][...]
    for turn in range(groups):
        source = lax.rem(chip + groups - turn, groups)
        joined[:, turn * depth : (turn + 1) * depth] = held[group ^ source]
    rows = joined[...]
    mine = jnp.dot(rows, mine_ref[...], preferred_element_type=F32).astype(BF16)
    other = jnp.dot(rows, other_ref[...], preferred_element_type=F32).astype(BF16)

    @pl.when(core == 0)
    def _():
        out_ref[:, :width] = mine
        out_ref[:, width:] = other

    @pl.when(core != 0)
    def _():
        out_ref[:, :width] = other
        out_ref[:, width:] = mine


def output_product(attention, mine, other):
    groups = len(attention)
    rows, depth = attention[0].shape
    width = mine.shape[1]
    return pl.pallas_call(
        functools.partial(output_body, groups),
        out_shape=shape_of((rows, 2 * width), BF16),
        in_specs=[VMEM] * (groups + 2),
        out_specs=VMEM,
        scratch_shapes=[
            pltpu.VMEM((groups, rows, depth), BF16),
            pltpu.VMEM((rows, groups * depth), BF16),
        ],
        cost_estimate=cost(
            4 * rows * depth * groups * width, 4 * depth * groups * width + 4 * rows * width
        ),
        compiler_params=GRANT,
        name="output_product",
    )(*attention, mine, other)


def direct_output(devices, groups):
    return devices == 2 * groups and groups == 4


def send_output_weight(output_weight):
    groups = lax.axis_size("tp")

    def flat(chip, core, group):
        return (2 * chip + core) * groups + group

    pieces = []
    for turn in range(groups):
        pairs = [
            (flat(chip, core, group), flat((group + turn) % groups, core, chip))
            for chip in range(groups)
            for core in range(2)
            for group in range(groups)
        ]
        pieces.append(lax.ppermute(output_weight, ("grid", "tp"), pairs))
    return pieces


def local(latents, input_weight, norm_gains, text_pairs, text_count, output_weight):
    devices, groups = lax.axis_size("grid"), lax.axis_size("tp")
    direct = direct_output(devices, groups)
    if direct:
        pieces = send_output_weight(output_weight)
    query, pair = project(latents, input_weight, norm_gains)
    attention = attention_rows(query, pair, text_pairs, norm_gains, text_count)
    if not direct:
        weight = lax.all_gather(output_weight, "grid", axis=1, tiled=True)
        term = jnp.dot(attention, weight, preferred_element_type=F32)
        return lax.psum_scatter(term.astype(BF16), "tp", scatter_dimension=1, tiled=True)
    mine = jnp.concatenate(pieces, axis=0)
    other = lax.ppermute(mine, "grid", [(at, at ^ 1) for at in range(devices)])
    gathered = [attention] + [
        lax.ppermute(attention, "tp", [(at, at ^ by) for at in range(groups)])
        for by in range(1, groups)
    ]
    return output_product(gathered, mine, other)


def solution(mesh):
    placed = (P("grid", None), P("grid", "tp"), P(), P(None, "tp"), P(), P("tp", "grid"))
    return jax.shard_map(
        local, mesh=mesh, in_specs=placed, out_specs=P("grid", "tp"), check_vma=False
    )
```

```python
import functools

import jax
import jax.numpy as jnp
import numpy as np
from jax import lax
from jax.experimental import pallas as pl
from jax.experimental.pallas import tpu as pltpu
from jax.sharding import PartitionSpec as P


GRID_H = 4
LOG2E = float(np.log2(np.e))

epsilon = 1e-06


F32 = jnp.float32
BF16 = jnp.bfloat16
VMEM = pl.BlockSpec(memory_space=pltpu.VMEM)
SMEM = pl.BlockSpec(memory_space=pltpu.SMEM)
GRANT = pltpu.CompilerParams(vmem_limit_bytes=16 * 1024 * 1024)


def shape_of(shape, dtype):
    return jax.ShapeDtypeStruct(shape, dtype)


def cost(flops, bytes_accessed, transcendentals=0):
    return pl.CostEstimate(
        flops=int(flops), bytes_accessed=int(bytes_accessed), transcendentals=int(transcendentals)
    )


def root_norm(values, gain):
    return values * lax.rsqrt(jnp.mean(values * values, axis=-1, keepdims=True) + epsilon) * gain


def partial_body(slots, carried, latents_ref, partner_ref, *refs):
    chips = lax.axis_size("grid") // 2
    place = lax.axis_index("grid")
    chip, core = place // 2, lax.rem(place, 2)
    weights, refs = refs[: len(slots)], refs[len(slots) :]
    if carried:
        carried_mine, carried_other = refs[:2]
        refs = refs[2:]
    mine_ref, other_ref = refs
    depth = weights[0].shape[0]

    def products(weight_ref, owner):
        columns = pl.ds(pl.multiple_of((2 * owner + core) * depth, depth), depth)
        weight = weight_ref[...]
        return (
            jnp.dot(latents_ref[:, columns], weight, preferred_element_type=F32),
            jnp.dot(partner_ref[:, columns], weight, preferred_element_type=F32),
        )

    mine = other = None
    if carried:
        mine, other = carried_mine[...], carried_other[...]
    for weight_ref, (owner_of, here) in zip(weights, slots):
        if here is None:
            add_mine, add_other = products(weight_ref, owner_of(chip))
            mine = add_mine if mine is None else mine + add_mine
            other = add_other if other is None else other + add_other
    mine_ref[...], other_ref[...] = mine, other
    for weight_ref, (owner_of, here) in zip(weights, slots):
        if here is not None:

            @pl.when(here(chip, chips))
            def _():
                add_mine, add_other = products(weight_ref, owner_of(chip))
                mine_ref[...] += add_mine
                other_ref[...] += add_other


def partial_product(latents, partner_latents, weights, slots, carry):
    rows = latents.shape[0]
    depth, width = weights[0].shape
    count = len(weights)
    carry = list(carry)
    return pl.pallas_call(
        functools.partial(partial_body, tuple(slots), bool(carry)),
        out_shape=[shape_of((rows, width), F32)] * 2,
        in_specs=[VMEM] * (2 + count + len(carry)),
        out_specs=[VMEM] * 2,
        cost_estimate=cost(4 * rows * depth * width * count, 4 * rows * depth * count),
        compiler_params=GRANT,
        name="partial_product",
    )(latents, partner_latents, *weights, *carry)


def keys_body(head_size, mine_ref, other_ref, gains_ref, pair_ref):
    total = mine_ref[...] + other_ref[...]
    keys = root_norm(total[:, :head_size], gains_ref[1:2])
    pair_ref[:, :head_size] = keys.astype(BF16)
    pair_ref[:, head_size:] = total[:, head_size:].astype(BF16)


def query_body(mine_ref, other_ref, gains_ref, query_ref):
    query_ref[...] = root_norm(mine_ref[...] + other_ref[...], gains_ref[0:1]).astype(BF16)


def finish(body, mine, other, norm_gains):
    rows, width = mine.shape
    return pl.pallas_call(
        body,
        out_shape=shape_of((rows, width), BF16),
        in_specs=[VMEM] * 3,
        out_specs=VMEM,
        cost_estimate=cost(10 * rows * width, 10 * rows * width, rows),
        compiler_params=GRANT,
    )(mine, other, norm_gains)


def filled(pairs, devices):
    sources, targets = {at for at, _ in pairs}, {to for _, to in pairs}
    return pairs + [(at, at) for at in range(devices) if at not in sources | targets]


def project(latents, input_weight, norm_gains):
    devices = lax.axis_size("grid")
    chips = devices // 2
    head_size = norm_gains.shape[1]
    finish_keys = functools.partial(keys_body, head_size)
    if devices % 2 or chips != 4:
        weight = lax.all_gather(input_weight, "grid", axis=0, tiled=True)
        total = jnp.dot(latents, weight, preferred_element_type=F32)
        zero = jnp.zeros_like(total)
        query = finish(query_body, total[:, :head_size], zero[:, :head_size], norm_gains)
        pair = finish(finish_keys, total[:, head_size:], zero[:, head_size:], norm_gains)
        return query, pair
    every = range(devices)
    swap = [(at, at ^ 1) for at in every]
    across = [(at, at ^ chips) for at in every]
    beside = [(at, at ^ 2) for at in every]
    half = chips // 2
    pair_weight, query_weight = input_weight[:, head_size:], input_weight[:, :head_size]
    far = lax.ppermute(pair_weight, "grid", across)
    near = lax.ppermute(pair_weight, "grid", beside)
    partner_latents = lax.ppermute(latents, "grid", swap)
    relayed = lax.ppermute(far, "grid", beside)
    query_shards = [query_weight] + [
        lax.ppermute(query_weight, "grid", [(at, (at + 2 * turn) % devices) for at in every])
        for turn in range(1, chips)
    ]
    carry = partial_product(
        latents,
        partner_latents,
        [pair_weight, far, near],
        [(lambda chip: chip, None), (lambda chip: chip ^ half, None), (lambda chip: chip ^ 1, None)],
        (),
    )
    mine, other = partial_product(
        latents, partner_latents, [relayed], [(lambda chip: chip ^ half ^ 1, None)], carry
    )
    pair = finish(finish_keys, mine, lax.ppermute(other, "grid", swap), norm_gains)
    mine, other = partial_product(
        latents,
        partner_latents,
        query_shards,
        [
            (lambda chip, turn=turn: lax.rem(chip + chips - turn, chips), None)
            for turn in range(chips)
        ],
        (),
    )
    query = finish(query_body, mine, lax.ppermute(other, "grid", swap), norm_gains)
    return query, pair


def attend(state, query, tiles, factor):
    rows, head_size = query.shape
    scores = []
    for keys, _, live in tiles:
        score = lax.dot_general(query, keys, (((1,), (1,)), ((), ())), preferred_element_type=F32)
        for at in range(0, keys.shape[0], head_size):
            part = score[:, at : at + head_size]
            if live is not None:
                part = jnp.where(live[:, at : at + head_size], part, -jnp.inf)
            scores.append(part)
    top = functools.reduce(jnp.maximum, scores).max(-1, keepdims=True)
    top = jnp.broadcast_to(top, (rows, head_size)) * factor
    if state is not None:
        top = jnp.maximum(state[0], top)
    mixed = None
    at = 0
    for keys, values, _ in tiles:
        count = keys.shape[0] // head_size
        weights = [jnp.exp2(part * factor - top).astype(BF16) for part in scores[at : at + count]]
        at += count
        wide = jnp.concatenate([values, jnp.ones_like(values)], axis=1)
        add = jnp.dot(jnp.concatenate(weights, axis=1), wide, preferred_element_type=F32)
        mixed = add if mixed is None else mixed + add
    total, mixed = mixed[:, head_size:], mixed[:, :head_size]
    if state is not None:
        fade = jnp.exp2(state[0] - top)
        total, mixed = state[1] * fade + total, state[2] * fade + mixed
    return top, total, mixed


def outer_height(height):
    return jnp.where(lax.rem(height, 2) == 0, height - 1, height + 1)


def attend_body(slots, with_text, carried, last, factor, *refs):
    place = lax.axis_index("grid")
    times = lax.axis_size("grid") // GRID_H
    time, height = place // GRID_H, lax.rem(place, GRID_H)
    beyond = outer_height(height)
    outer_ok = (beyond >= 0) & (beyond < GRID_H)
    query_ref, refs = refs[0], refs[1:]
    pair_refs, refs = refs[: len(slots)], refs[len(slots) :]
    head_size = query_ref.shape[1]
    rows = query_ref.shape[0]
    if with_text:
        count_ref, text_ref, gains_ref = refs[:3]
        refs = refs[3:]
    if carried:
        carry, refs = refs[:3], refs[3:]
    held = refs[1:] if last else refs
    out_ref = refs[0]

    def before():
        return tuple(ref[...] for ref in carry) if carried else None

    def tiles_of(which):
        return [
            (pair_refs[at][:, :head_size], pair_refs[at][:, head_size:], None) for at in which
        ]

    def keep(state):
        held[0][...], held[1][...], held[2][...] = state

    def finish(state):
        if last:
            out_ref[...] = (state[2] / state[1]).astype(BF16)
        else:
            keep(state)

    always = [at for at, (by, outer) in enumerate(slots) if by is None and not outer]
    sometimes = [at for at in range(len(slots)) if at not in always]
    if all(slots[at][0] is None for at in sometimes):
        if with_text:
            text_keys = root_norm(text_ref[:, :head_size].astype(F32), gains_ref[1:2]).astype(BF16)
            live = lax.broadcasted_iota(jnp.int32, (rows, text_ref.shape[0]), 1) < count_ref[0]
            extra = [(text_keys, text_ref[:, head_size:], live)]
        else:
            extra = []
        if not sometimes:
            finish(attend(before(), query_ref[...], extra + tiles_of(always), factor))
            return

        @pl.when(outer_ok)
        def _():
            both = extra + tiles_of(always + sometimes)
            finish(attend(before(), query_ref[...], both, factor))

        @pl.when(jnp.logical_not(outer_ok))
        def _():
            some = extra + tiles_of(always)
            finish(attend(before(), query_ref[...], some, factor) if some else before())

        return
    keep(before())
    for at in range(len(slots)):
        by, outer = slots[at]
        gate = (time - by >= 0) & (time - by < times)
        gate = gate & outer_ok if outer else gate

        @pl.when(gate)
        def _():
            state = held[0][...], held[1][...], held[2][...]
            keep(attend(state, query_ref[...], tiles_of([at]), factor))

    if last:
        finish((held[0][...], held[1][...], held[2][...]))


def attention_step(query, pairs, slots, text=(), carry=(), last=False):
    rows, head_size = query.shape
    factor = head_size ** (-0.5) * LOG2E
    text, carry = list(text), list(carry)
    plane = shape_of((rows, head_size), F32)
    columns = sum(pair.shape[0] for pair in pairs)
    return pl.pallas_call(
        functools.partial(attend_body, tuple(slots), bool(text), bool(carry), last, factor),
        out_shape=shape_of((rows, head_size), BF16) if last else [plane] * 3,
        in_specs=[VMEM] * (1 + len(pairs))
        + ([SMEM, VMEM, VMEM] if text else [])
        + [VMEM] * len(carry),
        out_specs=VMEM if last else [VMEM] * 3,
        scratch_shapes=[pltpu.VMEM((rows, head_size), F32)] * 3 if last else [],
        cost_estimate=cost(4 * rows * columns * head_size, 4 * columns * head_size, rows * columns),
        compiler_params=GRANT,
        name="attention_step",
    )(query, *pairs, *text, *carry)


def reply_body(query_ref, own_ref, partner_ref, outer_ref, out_ref, *, factor):
    rows, head_size = query_ref.shape
    beyond = outer_height(lax.rem(lax.axis_index("grid"), GRID_H))
    outer_ok = (beyond >= 0) & (beyond < GRID_H)

    def tiles(refs):
        return [(ref[:, :head_size], ref[:, head_size:], None) for ref in refs]

    def finish(refs):
        top, total, mixed = attend(None, query_ref[...], tiles(refs), factor)
        out_ref[:rows] = (mixed / total).astype(BF16)
        level = top + jnp.log(total) * LOG2E
        square = (head_size, head_size)
        diagonal = lax.broadcasted_iota(jnp.int32, square, 0) == lax.broadcasted_iota(
            jnp.int32, square, 1
        )
        tail = (out_ref.shape[0] - rows, head_size)
        line = lax.broadcasted_iota(jnp.int32, tail, 0)
        terms = jnp.zeros(tail, F32)
        for at in range(rows // head_size):
            block = level[at * head_size : (at + 1) * head_size]
            rest = jnp.where(diagonal, block, 0.0).sum(0, keepdims=True)
            for part in range(3):
                term = rest.astype(BF16).astype(F32)
                terms = jnp.where(line == 3 * at + part, term, terms)
                rest = rest - term
        out_ref[rows:] = terms.astype(BF16)

    @pl.when(outer_ok)
    def _():
        finish([own_ref, partner_ref, outer_ref])

    @pl.when(jnp.logical_not(outer_ok))
    def _():
        finish([own_ref, partner_ref])


def reply(query, tiles):
    rows, head_size = query.shape
    tail = -(-3 * (rows // head_size) // 16) * 16
    return pl.pallas_call(
        functools.partial(reply_body, factor=head_size ** (-0.5) * LOG2E),
        out_shape=shape_of((rows + tail, head_size), BF16),
        in_specs=[VMEM] * (1 + len(tiles)),
        out_specs=VMEM,
        cost_estimate=cost(12 * rows * rows * head_size, 8 * rows * head_size, 3 * rows * rows),
        compiler_params=GRANT,
        name="reply",
    )(query, *tiles)


def merge_body(top_ref, total_ref, mixed_ref, reply_ref, out_ref):
    rows, head_size = out_ref.shape
    terms = reply_ref[rows:].astype(F32)
    for at in range(rows // head_size):
        here = slice(at * head_size, (at + 1) * head_size)
        line = terms[3 * at : 3 * at + 1] + terms[3 * at + 1 : 3 * at + 2]
        line = line + terms[3 * at + 2 : 3 * at + 3]
        level = jnp.transpose(jnp.broadcast_to(line, (head_size, head_size)))
        top = jnp.maximum(top_ref[here], level)
        mine, theirs = jnp.exp2(top_ref[here] - top), jnp.exp2(level - top)
        mixed = mixed_ref[here] * mine + reply_ref[here].astype(F32) * theirs
        out_ref[here] = (mixed / (total_ref[here] * mine + theirs)).astype(BF16)


def merge(state, replied):
    rows, head_size = state[2].shape
    return pl.pallas_call(
        merge_body,
        out_shape=shape_of((rows, head_size), BF16),
        in_specs=[VMEM] * 4,
        out_specs=VMEM,
        cost_estimate=cost(8 * rows * head_size, 16 * rows * head_size, 2 * rows),
        compiler_params=GRANT,
        name="merge",
    )(*state, replied)


def attention_rows(query, pair, text_pairs, norm_gains, text_count):
    devices = lax.axis_size("grid")
    times = devices // GRID_H
    swap = [(at, at ^ 1) for at in range(devices)]
    outer = []
    for at in range(devices):
        row = at % GRID_H
        beyond = row - 1 if row % 2 == 0 else row + 1
        if 0 <= beyond < GRID_H:
            outer.append((at, at - row + beyond))

    def later(pairs, by):
        return [(at, to + by * GRID_H) for at, to in pairs if 0 <= to + by * GRID_H < devices]

    same = [(at, at) for at in range(devices)]
    if times == 2:
        half = devices // 2
        plans = [(None, [(at, at ^ half) for at in range(devices)], [(at, to ^ half) for at, to in outer])]
    elif times > 2:
        plans = [(by, later(same, by), later(outer, by)) for by in (1, -1)]
    else:
        plans = []
    if times == 2:
        across = plans[0][1]
        asked = lax.ppermute(query, "grid", across)
        partner = lax.ppermute(pair, "grid", swap)
        near_outer = lax.ppermute(pair, "grid", filled(outer, devices))
        tiles = [pair, partner, near_outer]
        replied = lax.ppermute(reply(asked, tiles), "grid", across)
        state = attention_step(
            query,
            tiles,
            [(None, False), (None, False), (None, True)],
            text=(text_count, text_pairs, norm_gains),
        )
        return merge(state, replied)
    far = [lax.ppermute(pair, "grid", along) for _, along, _ in plans]
    partner = lax.ppermute(pair, "grid", swap)
    near_outer = lax.ppermute(pair, "grid", filled(outer, devices))
    far_outer = [lax.ppermute(pair, "grid", filled(over, devices)) for _, _, over in plans]
    text = (text_count, text_pairs, norm_gains)
    carry = attention_step(query, [pair, partner], [(None, False), (None, False)], text=text)
    if not plans:
        return attention_step(query, [near_outer], [(None, True)], carry=carry, last=True)
    for at, (by, _, _) in enumerate(plans):
        far_partner = lax.ppermute(far[at], "grid", swap)
        near, near_slots = ([near_outer], [(None, True)]) if by is None else ([], [])
        if by is not None and at == 0:
            carry = attention_step(query, [near_outer], [(None, True)], carry=carry)
        carry = attention_step(query, [far[at], *near], [(by, False), *near_slots], carry=carry)
        carry = attention_step(
            query,
            [far_partner, far_outer[at]],
            [(by, False), (by, True)],
            carry=carry,
            last=at == len(plans) - 1,
        )
    return carry


def output_body(groups, *refs):
    attention, refs = refs[:groups], refs[groups:]
    mine_ref, other_ref, out_ref, held, joined = refs
    place, group = lax.axis_index("grid"), lax.axis_index("tp")
    chip, core = place // 2, lax.rem(place, 2)
    depth, width = mine_ref.shape[0] // groups, mine_ref.shape[1]
    for at in range(groups):
        held[at] = attention[at][...]
    for turn in range(groups):
        source = lax.rem(chip + groups - turn, groups)
        joined[:, turn * depth : (turn + 1) * depth] = held[group ^ source]
    rows = joined[...]
    mine = jnp.dot(rows, mine_ref[...], preferred_element_type=F32).astype(BF16)
    other = jnp.dot(rows, other_ref[...], preferred_element_type=F32).astype(BF16)

    @pl.when(core == 0)
    def _():
        out_ref[:, :width] = mine
        out_ref[:, width:] = other

    @pl.when(core != 0)
    def _():
        out_ref[:, :width] = other
        out_ref[:, width:] = mine


def output_product(attention, mine, other):
    groups = len(attention)
    rows, depth = attention[0].shape
    width = mine.shape[1]
    return pl.pallas_call(
        functools.partial(output_body, groups),
        out_shape=shape_of((rows, 2 * width), BF16),
        in_specs=[VMEM] * (groups + 2),
        out_specs=VMEM,
        scratch_shapes=[
            pltpu.VMEM((groups, rows, depth), BF16),
            pltpu.VMEM((rows, groups * depth), BF16),
        ],
        cost_estimate=cost(
            4 * rows * depth * groups * width, 4 * depth * groups * width + 4 * rows * width
        ),
        compiler_params=GRANT,
        name="output_product",
    )(*attention, mine, other)


def direct_output(devices, groups):
    return devices == 2 * groups and groups == 4


def send_output_weight(output_weight):
    groups = lax.axis_size("tp")

    def flat(chip, core, group):
        return (2 * chip + core) * groups + group

    pieces = []
    for turn in range(groups):
        pairs = [
            (flat(chip, core, group), flat((group + turn) % groups, core, chip))
            for chip in range(groups)
            for core in range(2)
            for group in range(groups)
        ]
        pieces.append(lax.ppermute(output_weight, ("grid", "tp"), pairs))
    return pieces


def local(latents, input_weight, norm_gains, text_pairs, text_count, output_weight):
    devices, groups = lax.axis_size("grid"), lax.axis_size("tp")
    direct = direct_output(devices, groups)
    if direct:
        pieces = send_output_weight(output_weight)
    query, pair = project(latents, input_weight, norm_gains)
    attention = attention_rows(query, pair, text_pairs, norm_gains, text_count)
    if not direct:
        weight = lax.all_gather(output_weight, "grid", axis=1, tiled=True)
        term = jnp.dot(attention, weight, preferred_element_type=F32)
        return lax.psum_scatter(term.astype(BF16), "tp", scatter_dimension=1, tiled=True)
    mine = jnp.concatenate(pieces, axis=0)
    other = lax.ppermute(mine, "grid", [(at, at ^ 1) for at in range(devices)])
    gathered = [attention] + [
        lax.ppermute(attention, "tp", [(at, at ^ by) for at in range(groups)])
        for by in range(1, groups)
    ]
    return output_product(gathered, mine, other)


def solution(mesh):
    placed = (P("grid", None), P("grid", "tp"), P(), P(None, "tp"), P(), P("tp", "grid"))
    return jax.shard_map(
        local, mesh=mesh, in_specs=placed, out_specs=P("grid", "tp"), check_vma=False
    )
```
